32 devices in a mesh: sub: 4 (over y, core), row: 2 (over x), col: 4 (over z).
Axes of the slice: x: 2, y: 2, z: 4, core: 2. Of those that a mesh axis runs over, the one named last changes fastest.
Arguments:
- inverse_quarter: bfloat16 [4, 8192, 8192], P('sub', 'row', 'col'), may hold values from -1 to 3
- inverse_half: bfloat16 [4, 8192, 4096], P('sub', 'row', 'col'), may hold values from -1 to 3
- inverse_root: bfloat16 [16384, 16384], P('row', ('sub', 'col')), may hold values from -1 to 3
- quarter_to_half: bfloat16 [4, 2, 4096, 8192], P('sub', None, 'col', 'row'), may hold values from -0.0625 to 0.0625
- quarter_to_root: bfloat16 [4, 2, 4096, 8192], P('sub', None, 'col', 'row'), may hold values from -0.0625 to 0.0625
- half_to_root: bfloat16 [4, 2, 4096, 8192], P('sub', None, 'col', 'row'), may hold values from -0.0625 to 0.0625
- right_quarter: bfloat16 [4, 8192, 256], P('sub', 'col'), may hold values from -6 to 6
- right_half: bfloat16 [4, 4096, 256], P('sub', 'col'), may hold values from -6 to 6
- right_root: bfloat16 [16384, 256], P(('sub', 'col')), may hold values from -6 to 6
- row_blocks: int32 [3, 4, 2, 16], replicated, may hold values 0 or 1
Outputs:
- quarter_solution: float32 [4, 8192, 256], P('sub', 'col', 'row')
- half_solution: bfloat16 [4, 4096, 256], P('sub', 'col')
- root_solution: bfloat16 [16384, 256], P(('sub', 'col'))
The draws below stay inside these ranges and needn't reach their ends.
All inputs are finite; a program needn't handle non-finite values.
Results may differ from the reference program's by a relative error of at most 0.01.
Values may be sent and summed in bfloat16 or wider, within the bound.
No kernel may reach another device: no remote copies, remote signals or barrier semaphores. Data moves between devices by JAX's collectives and lax.ppermute only.
A program may use at most 256 MiB of HBM per device.

```python
import math
import jax
import jax.numpy as jnp
from jax import lax

SQ = 8192
SH = 8192
SR = 16384
NRHS = 256
BLK = 256


def dominant(key, shape, order, on_diagonal):
    first_key, second_key = jax.random.split(key)
    spread = jax.random.truncated_normal(first_key, -6.0, 6.0, shape, jnp.float32)
    diagonal = jnp.exp(jax.random.uniform(second_key, shape, jnp.float32, 0.0, math.log(2.0)))
    return jnp.where(on_diagonal, diagonal, 0.0) + spread * (0.5 / math.sqrt(order))


def draw_inverse_quarter(key, part):
    shape = (4, SQ, SQ)
    on_diagonal = lax.broadcasted_iota(jnp.int32, shape, 1) == lax.broadcasted_iota(jnp.int32, shape, 2)
    return dominant(jax.random.fold_in(key, 11), shape, SQ, on_diagonal).astype(jnp.bfloat16)


def draw_inverse_half(key, part):
    shape = (4, SH, SH // 2)
    offset = lax.broadcasted_iota(jnp.int32, shape, 0) % 2 * (SH // 2)
    on_diagonal = lax.broadcasted_iota(jnp.int32, shape, 1) == offset + lax.broadcasted_iota(jnp.int32, shape, 2)
    return dominant(jax.random.fold_in(key, 12), shape, SH, on_diagonal).astype(jnp.bfloat16)


def draw_inverse_root(key, part):
    shape = (SR, SR)
    on_diagonal = lax.broadcasted_iota(jnp.int32, shape, 0) == lax.broadcasted_iota(jnp.int32, shape, 1)
    return dominant(jax.random.fold_in(key, 13), shape, SR, on_diagonal).astype(jnp.bfloat16)


def set_ends(array, stream_key, smallest, high):
    spot = [jax.random.randint(jax.random.fold_in(stream_key, axis), (), 0, length) for axis, length in enumerate(array.shape)]
    longest = array.shape.index(max(array.shape))
    next_to = spot[:longest] + [(spot[longest] + 1) % array.shape[longest]] + spot[longest + 1:]
    return array.at[tuple(spot)].set(smallest).at[tuple(next_to)].set(high)


def block_scale(key, shape, shards, least, high):
    gain, own = 1.0, jax.random.fold_in(key, 6)
    for axis_at, shards_of in shards:
        heights = jnp.exp(jax.random.uniform(jax.random.fold_in(own, axis_at), (shards_of,), jnp.float32, least / len(shards), high / len(shards)))
        gain = gain * jnp.repeat(heights, shape[axis_at] // shards_of).reshape([-1 if axis == axis_at else 1 for axis in range(len(shape))])
    return gain


def gaussian(stream_key, dims, width, reach, shards=(), held_as=jnp.bfloat16):
    factor_of = block_scale(stream_key, dims, shards, -0.22, 0.18) if shards else 1.0
    entries = jax.random.normal(stream_key, dims, jnp.float32) * width * factor_of
    return jnp.minimum(jnp.maximum(entries, -reach), reach).astype(held_as)


def setup_inputs(seed: int = 0) -> dict:
    arg_keys = jax.random.split(jax.random.key(seed), 11)
    inverse_quarter = draw_inverse_quarter(jax.random.fold_in(arg_keys[10], 71), 0)
    inverse_half = draw_inverse_half(jax.random.fold_in(arg_keys[10], 71), 0)
    inverse_root = draw_inverse_root(jax.random.fold_in(arg_keys[10], 71), 0)
    quarter_to_half = gaussian(arg_keys[3], (4, 2, SH // 2, SQ), SQ ** -0.5, 0.0625, ((0, 4), (2, 4), (3, 2)))
    quarter_to_root = gaussian(arg_keys[4], (4, 2, SR // 4, SQ), SQ ** -0.5, 0.0625, ((0, 4), (2, 4), (3, 2)))
    half_to_root = gaussian(arg_keys[5], (4, 2, SR // 4, SH), SH ** -0.5, 0.0625, ((0, 4), (2, 4), (3, 2)))
    right_quarter = gaussian(arg_keys[6], (4, SQ, NRHS), 1.0, 6.0, ((0, 4), (1, 4)))
    right_half = gaussian(arg_keys[7], (4, SH // 2, NRHS), 1.0, 6.0, ((0, 4), (1, 4)))
    right_root = gaussian(arg_keys[8], (SR, NRHS), 1.0, 6.0, ((0, 16),))
    row_blocks = set_ends((jax.random.randint(arg_keys[9], (3, 4, 2, SH // (2 * BLK)), 0, 4) < 3).astype(jnp.int32), jax.random.fold_in(arg_keys[9], 1), 0, 1)
    return {"inverse_quarter": inverse_quarter, "inverse_half": inverse_half, "inverse_root": inverse_root, "quarter_to_half": quarter_to_half, "quarter_to_root": quarter_to_root, "half_to_root": half_to_root, "right_quarter": right_quarter, "right_half": right_half, "right_root": right_root, "row_blocks": row_blocks}


def expand_flags(flags):
    return jnp.repeat(flags, BLK, axis=1).astype(jnp.float32)


def project(matrix, vector):
    halves, height, inner = matrix.shape
    flat = jnp.dot(matrix.reshape(halves * height, inner), vector, preferred_element_type=jnp.float32)
    return flat.reshape(halves, height, vector.shape[1])


def project_back(matrix, pieces):
    inner = matrix.shape[2]
    return lax.dot_general(matrix.reshape(-1, inner), pieces.reshape(-1, pieces.shape[2]), (((0,), (0,)), ((), ())), preferred_element_type=jnp.float32)


def transposed(matrix, vector):
    return lax.dot_general(matrix, vector, (((0,), (0,)), ((), ())), preferred_element_type=jnp.float32)


def reference(inverse_quarter, inverse_half, inverse_root, quarter_to_half, quarter_to_root, half_to_root, right_quarter, right_half, right_root, row_blocks):
    masking = [[expand_flags(row_blocks[kind, index])[:, :, None] for index in range(4)] for kind in range(3)]
    solved_quarter = [jnp.dot(inverse_quarter[index], right_quarter[index], preferred_element_type=jnp.float32).astype(jnp.bfloat16) for index in range(4)]
    half_matrix = [jnp.concatenate([inverse_half[2 * half], inverse_half[2 * half + 1]], axis=1) for half in range(2)]
    solved_half = []
    for half in range(2):
        update = jnp.concatenate([right_half[2 * half], right_half[2 * half + 1]], axis=0).astype(jnp.float32)
        for side in range(2):
            index = 2 * half + side
            term = project(quarter_to_half[index], solved_quarter[index]) * masking[0][index]
            update = update - term.reshape(SH, NRHS)
        solved_half.append(jnp.dot(half_matrix[half], update.astype(jnp.bfloat16), preferred_element_type=jnp.float32).astype(jnp.bfloat16))
    root_terms = jnp.zeros((4, SR // 4, NRHS), jnp.float32)
    for index in range(4):
        half = index // 2
        side = index % 2
        term = project(quarter_to_root[index], solved_quarter[index]) * masking[1][index]
        term = term + project(half_to_root[index], solved_half[half]) * masking[2][index]
        root_terms = root_terms.at[side].add(term[0]).at[2 + side].add(term[1])
    root_right = (right_root.astype(jnp.float32) - root_terms.reshape(SR, NRHS)).astype(jnp.bfloat16)
    solved_root = jnp.dot(inverse_root, root_right, preferred_element_type=jnp.float32).astype(jnp.bfloat16)
    root_solution = transposed(inverse_root, solved_root).astype(jnp.bfloat16)
    root_blocks = root_solution.reshape(4, SR // 4, NRHS)
    half_out = []
    quarter_out = []
    for half in range(2):
        update = solved_half[half].astype(jnp.float32)
        for side in range(2):
            index = 2 * half + side
            pieces = jnp.stack([root_blocks[side], root_blocks[2 + side]])
            update = update - project_back(half_to_root[index], pieces * masking[2][index].astype(jnp.bfloat16))
        half_result = transposed(half_matrix[half], update.astype(jnp.bfloat16)).astype(jnp.bfloat16)
        half_pieces = half_result.reshape(2, SH // 2, NRHS)
        half_out.append(half_pieces)
        for side in range(2):
            index = 2 * half + side
            pieces = jnp.stack([root_blocks[side], root_blocks[2 + side]])
            quarter_update = solved_quarter[index].astype(jnp.float32)
            quarter_update = quarter_update - project_back(quarter_to_half[index], half_pieces * masking[0][index].astype(jnp.bfloat16))
            quarter_update = quarter_update - project_back(quarter_to_root[index], pieces * masking[1][index].astype(jnp.bfloat16))
            quarter_out.append(transposed(inverse_quarter[index], quarter_update.astype(jnp.bfloat16)))
    return jnp.stack(quarter_out), jnp.concatenate(half_out, axis=0), root_solution
```

```python
import jax
import jax.numpy as jnp
from jax import lax
from jax.sharding import PartitionSpec as P

BLK = 256
STREAMS = 1
F32 = jnp.float32
BF16 = jnp.bfloat16


def swap(values, axis, distance):
    pairs = [(i, i ^ distance) for i in range(lax.axis_size(axis))]
    return lax.ppermute(values, axis, pairs)


def pick(values, index):
    return lax.dynamic_index_in_dim(values, index, 0, keepdims=False)


def is_power_of_two(count):
    return count & (count - 1) == 0


def scatter_sum(partial, axis):
    count = lax.axis_size(axis)
    own = lax.axis_index(axis)
    pieces = partial.reshape(count, partial.shape[0] // count, partial.shape[1])
    total = pick(pieces, own)
    for distance in range(1, count):
        total = total + swap(pick(pieces, own ^ distance).astype(BF16), axis, distance).astype(F32)
    return total


def gather(piece, axis):
    count = lax.axis_size(axis)
    own = lax.axis_index(axis)
    whole = jnp.zeros((count,) + piece.shape, piece.dtype)
    whole = lax.dynamic_update_index_in_dim(whole, piece, own, 0)
    for distance in range(1, count):
        whole = lax.dynamic_update_index_in_dim(
            whole, swap(piece, axis, distance), own ^ distance, 0
        )
    return whole.reshape((count * piece.shape[0],) + piece.shape[1:])


def pair_scatter(halves, bit_value, axis, distance):
    own_piece = pick(halves, bit_value)
    other_piece = pick(halves, 1 - bit_value)
    return own_piece + swap(other_piece.astype(BF16), axis, distance).astype(F32)


def pair_gather(piece, bit_value, axis, distance):
    other = swap(piece, axis, distance)
    return jnp.where(bit_value == 0, jnp.stack([piece, other]), jnp.stack([other, piece]))


def sum_rows(values):
    if lax.axis_size("row") != 2:
        return lax.psum(values, "row")
    sent = values.astype(BF16)
    return sent.astype(F32) + swap(sent, "row", 1).astype(F32)


def project(matrix, vector):
    halves, height, inner = matrix.shape
    flat = jnp.dot(
        matrix.reshape(halves * height, inner), vector, preferred_element_type=F32
    )
    return flat.reshape(halves, height, vector.shape[1])


def transposed(matrix, vector):
    return lax.dot_general(
        matrix, vector, (((0,), (0,)), ((), ())), preferred_element_type=F32
    )


def project_back(matrix, pieces):
    return transposed(
        matrix.reshape(-1, matrix.shape[2]), pieces.reshape(-1, pieces.shape[2])
    )


def halve(values):
    return values.reshape(2, values.shape[0] // 2, values.shape[1])


def join(values):
    return values.reshape(-1, values.shape[2])


def final_sum(values):
    if lax.axis_size("row") != 2:
        return lax.psum_scatter(values, "row", scatter_dimension=1, tiled=True)
    own = lax.axis_index("row")
    width = values.shape[1] // 2
    mine = lax.dynamic_slice_in_dim(values, own * width, width, 1)
    sent = lax.dynamic_slice_in_dim(values, (1 - own) * width, width, 1)
    return mine + swap(sent.astype(BF16), "row", 1).astype(F32)


def solve(
    inverse_quarter,
    inverse_half,
    inverse_root,
    quarter_to_half,
    quarter_to_root,
    half_to_root,
    right_quarter,
    right_half,
    right_root,
    masking,
):
    sub_index = lax.axis_index("sub")
    low_bit = sub_index % 2
    high_bit = sub_index // 2
    mask_half, mask_root, mask_upper = masking[0], masking[1], masking[2]

    quarter_partial = jnp.dot(inverse_quarter, right_quarter, preferred_element_type=F32)
    quarter_piece = scatter_sum(quarter_partial, "col").astype(BF16)
    solved_quarter = gather(quarter_piece, "col")

    half_part = project(quarter_to_half, solved_quarter) * mask_half
    half_terms = sum_rows(pair_scatter(half_part, low_bit, "sub", 1))
    half_right = (right_half.astype(F32) - half_terms).astype(BF16)
    root_part = project(quarter_to_root, solved_quarter) * mask_root

    half_partial = jnp.dot(inverse_half, half_right, preferred_element_type=F32)
    half_partial = pair_scatter(halve(half_partial), low_bit, "sub", 1)
    half_piece = scatter_sum(half_partial, "col").astype(BF16)
    solved_half = join(pair_gather(gather(half_piece, "col"), low_bit, "sub", 1))

    upper_part = project(half_to_root, solved_half) * mask_upper
    root_terms = sum_rows(pair_scatter(upper_part + root_part, high_bit, "sub", 2))
    root_right = (right_root.astype(F32) - root_terms).astype(BF16)

    root_partial = jnp.dot(inverse_root, root_right, preferred_element_type=F32)
    root_partial = pair_scatter(halve(root_partial), low_bit, "sub", 1)
    root_partial = pair_scatter(halve(root_partial), high_bit, "sub", 2)
    root_piece = scatter_sum(root_partial, "col").astype(BF16)
    solved_root = join(pair_gather(gather(root_piece, "col"), high_bit, "sub", 2))
    solved_root = join(pair_gather(solved_root, low_bit, "sub", 1))

    root_solution = sum_rows(transposed(inverse_root, solved_root)).astype(BF16)
    root_pieces = pair_gather(root_solution, high_bit, "sub", 2)

    upper_back = project_back(half_to_root, root_pieces * mask_upper.astype(BF16))
    upper_back = pair_scatter(halve(upper_back), low_bit, "sub", 1)
    upper_total = scatter_sum(upper_back, "col")
    half_update_piece = (half_piece.astype(F32) - upper_total).astype(BF16)
    half_update = join(pair_gather(gather(half_update_piece, "col"), low_bit, "sub", 1))
    quarter_back = project_back(quarter_to_root, root_pieces * mask_root.astype(BF16))

    half_solution = sum_rows(transposed(inverse_half, half_update)).astype(BF16)
    half_pieces = pair_gather(half_solution, low_bit, "sub", 1)

    quarter_back = quarter_back + project_back(
        quarter_to_half, half_pieces * mask_half.astype(BF16)
    )
    quarter_total = scatter_sum(quarter_back, "col")
    quarter_update_piece = (quarter_piece.astype(F32) - quarter_total).astype(BF16)
    quarter_update = gather(quarter_update_piece, "col")
    return transposed(inverse_quarter, quarter_update), half_solution, root_solution


def per_device(
    inverse_quarter,
    inverse_half,
    inverse_root,
    quarter_to_half,
    quarter_to_root,
    half_to_root,
    right_quarter,
    right_half,
    right_root,
    row_blocks,
):
    sub_index = lax.axis_index("sub")
    column_index = lax.axis_index("col")
    block_count = quarter_to_half.shape[2] // BLK
    row_flags = lax.dynamic_slice(
        row_blocks,
        (jnp.int32(0), sub_index, jnp.int32(0), column_index * block_count),
        (3, 1, 2, block_count),
    )[:, 0]
    masking = jnp.repeat(row_flags, BLK, axis=2).astype(F32)[:, :, :, None]
    width = right_root.shape[1] // STREAMS
    outs = []
    for stream in range(STREAMS):
        columns = slice(stream * width, (stream + 1) * width)
        outs.append(
            solve(
                inverse_quarter[0],
                inverse_half[0],
                inverse_root,
                quarter_to_half[0],
                quarter_to_root[0],
                half_to_root[0],
                right_quarter[0][:, columns],
                right_half[0][:, columns],
                right_root[:, columns],
                masking,
            )
        )
    quarter, half, root = (
        parts[0] if STREAMS == 1 else jnp.concatenate(parts, axis=1) for parts in zip(*outs)
    )
    return (final_sum(quarter)[None], half[None], root)


def solution(mesh):
    placed = (
        P("sub", "row", "col"),
        P("sub", "row", "col"),
        P("row", ("sub", "col")),
        P("sub", None, "col", "row"),
        P("sub", None, "col", "row"),
        P("sub", None, "col", "row"),
        P("sub", "col", None),
        P("sub", "col", None),
        P(("sub", "col"), None),
        P(),
    )
    return jax.shard_map(
        per_device,
        mesh=mesh,
        in_specs=placed,
        out_specs=(P("sub", "col", "row"), P("sub", "col", None), P(("sub", "col"), None)),
        check_vma=False,
    )
```

```python
import jax
import jax.numpy as jnp
from jax import lax
from jax.experimental import pallas as pl
from jax.experimental.pallas import tpu as pltpu
from jax.sharding import PartitionSpec as P

BLK = 256
BLOCK_BYTES = 1 << 21
F32 = jnp.float32
BF16 = jnp.bfloat16


def swap(values, axis, distance):
    pairs = [(i, i ^ distance) for i in range(lax.axis_size(axis))]
    return lax.ppermute(values, axis, pairs)


def swap_core(values):
    return swap(values, "sub", 1)


def swap_y(values):
    return swap(values, "sub", 2)


def swap_z(values, distance):
    return swap(values, "col", distance)


def swap_x(values):
    return swap(values, "row", 1)


def multiply(matrix, vectors, in_blocks, order, outs, flags=None, addend=None):
    rows, inner = matrix.shape
    width = vectors[0].shape[1]
    tile = rows // order.shape[0]
    steps = order.shape[0]
    in_size = inner // in_blocks.shape[0]
    starts = [0]
    for out_rows, _ in outs:
        starts.append(starts[-1] + out_rows // tile)
    count = len(vectors)
    gathered = count > 1

    def body(places, visit, shown, *refs):
        vector_refs = refs[:count]
        matrix_ref = refs[count]
        addend_ref = refs[count + 1] if addend is not None else None
        out_refs = refs[count + 1 + (addend is not None) :][: len(outs)]
        step = pl.program_id(0)
        if gathered:
            x_ref = refs[-1]

            @pl.when(step == 0)
            def _():
                at = 0
                for ref in vector_refs:
                    for part in range(ref.shape[0] // in_size):
                        place = pl.multiple_of(places[at] * in_size, in_size)
                        x_ref[pl.ds(place, in_size), :] = ref[part * in_size : (part + 1) * in_size, :]
                        at += 1

        else:
            x_ref = vector_refs[0]
        total = jnp.dot(matrix_ref[...], x_ref[...], preferred_element_type=F32)
        if flags is not None:
            total = total * shown[visit[step]].astype(F32)
        if addend is not None:
            total = total + addend_ref[...]
        for index, ref in enumerate(out_refs):

            @pl.when((step >= starts[index]) & (step < starts[index + 1]))
            def _():
                ref[...] = total.astype(ref.dtype)

    def out_map(first, last):
        return lambda i, *_: (jnp.clip(i - first, 0, last - first - 1), 0)

    in_specs = [pl.BlockSpec(v.shape, lambda i, *_: (0, 0)) for v in vectors]
    in_specs.append(pl.BlockSpec((tile, inner), lambda i, places, visit, shown: (visit[i], 0)))
    operands = list(vectors) + [matrix]
    if addend is not None:
        in_specs.append(pl.BlockSpec((tile, width), lambda i, *_: (i, 0)))
        operands.append(addend)
    if flags is None:
        flags_operand = jnp.zeros((1,), jnp.int32)
    else:
        flags_operand = flags
    return pl.pallas_call(
        body,
        grid_spec=pltpu.PrefetchScalarGridSpec(
            num_scalar_prefetch=3,
            grid=(steps,),
            in_specs=in_specs,
            out_specs=[
                pl.BlockSpec((tile, width), out_map(starts[i], starts[i + 1]))
                for i in range(len(outs))
            ],
            scratch_shapes=[pltpu.VMEM((inner, width), BF16)] if gathered else [],
        ),
        out_shape=[jax.ShapeDtypeStruct((r, width), t) for r, t in outs],
        compiler_params=pltpu.CompilerParams(vmem_limit_bytes=40 << 20),
        cost_estimate=pl.CostEstimate(
            flops=2 * rows * inner * width,
            transcendentals=0,
            bytes_accessed=2 * rows * inner + 4 * (rows + inner) * width,
        ),
    )(in_blocks, order, flags_operand, *operands)


def multiply_back(matrix, vectors, in_blocks, order, outs, flags=None, addend=None, side=None):
    inner, columns = matrix.shape
    width = vectors[0].shape[0]
    steps = order.shape[0]
    tile = columns // steps
    in_size = inner // in_blocks.shape[0]
    mask_size = min(BLK, in_size)
    starts = [0]
    for out_columns, _ in outs:
        starts.append(starts[-1] + out_columns // tile)
    count = len(vectors)

    def body(places, visit, shown, *refs):
        vector_refs = refs[:count]
        matrix_ref = refs[count]
        addend_ref = refs[count + 1] if addend is not None else None
        y_ref = refs[-1]
        out_refs = refs[count + 1 + (addend is not None) : -1]
        step = pl.program_id(0)

        @pl.when(step == 0)
        def _():
            at = 0
            for ref in vector_refs:
                for part in range(ref.shape[1] // in_size):
                    if flags is None:
                        place = pl.multiple_of(places[at] * in_size, in_size)
                        y_ref[:, pl.ds(place, in_size)] = ref[:, part * in_size : (part + 1) * in_size]
                    else:
                        for inside in range(in_size // mask_size):
                            block = places[at] * (in_size // mask_size) + inside
                            place = pl.multiple_of(block * mask_size, mask_size)
                            start = part * in_size + inside * mask_size
                            held = ref[:, start : start + mask_size]
                            y_ref[:, pl.ds(place, mask_size)] = jnp.where(
                                shown[block] != 0, held, jnp.zeros_like(held)
                            )
                    at += 1

        total = jnp.dot(y_ref[...], matrix_ref[...], preferred_element_type=F32)
        if addend is not None:
            total = total + addend_ref[...]
        if side is not None:
            half = width // 2
            first = shown[0] == 0
            low, high = total[:half], total[half:]
            out_refs[0][...] = jnp.where(first, low, high).T
            out_refs[1][...] = jnp.where(first, high, low).T.astype(BF16)
            return
        for index, ref in enumerate(out_refs):

            @pl.when((step >= starts[index]) & (step < starts[index + 1]))
            def _():
                ref[...] = total.astype(ref.dtype)

    def out_map(first, last):
        return lambda i, *_: (0, jnp.clip(i - first, 0, last - first - 1))

    in_specs = [pl.BlockSpec(v.shape, lambda i, *_: (0, 0)) for v in vectors]
    in_specs.append(pl.BlockSpec((inner, tile), lambda i, places, visit, shown: (0, visit[i])))
    operands = list(vectors) + [matrix]
    if addend is not None:
        in_specs.append(pl.BlockSpec((width, tile), lambda i, *_: (0, i)))
        operands.append(addend)
    if side is not None:
        scalars = side[None]
        out_specs = [pl.BlockSpec((tile, width // 2), lambda i, *_: (i, 0))] * 2
        out_shape = [jax.ShapeDtypeStruct((columns, width // 2), t) for t in (F32, BF16)]
    else:
        scalars = jnp.zeros((1,), jnp.int32) if flags is None else flags
        out_specs = [
            pl.BlockSpec((width, tile), out_map(starts[i], starts[i + 1])) for i in range(len(outs))
        ]
        out_shape = [jax.ShapeDtypeStruct((width, c), t) for c, t in outs]
    return pl.pallas_call(
        body,
        grid_spec=pltpu.PrefetchScalarGridSpec(
            num_scalar_prefetch=3,
            grid=(steps,),
            in_specs=in_specs,
            out_specs=out_specs,
            scratch_shapes=[pltpu.VMEM((width, inner), BF16)],
        ),
        out_shape=out_shape,
        compiler_params=pltpu.CompilerParams(vmem_limit_bytes=40 << 20),
        cost_estimate=pl.CostEstimate(
            flops=2 * columns * inner * width,
            transcendentals=0,
            bytes_accessed=2 * columns * inner + 4 * (columns + inner) * width,
        ),
    )(in_blocks, order, scalars, *operands)


def listed(*values):
    return jnp.stack([jnp.asarray(v, jnp.int32) for v in values])


def spread(blocks, size, tile):
    parts = size // tile
    return (blocks[:, None] * parts + jnp.arange(parts, dtype=jnp.int32)[None]).reshape(-1)


def tile_of(piece, inner):
    return min(piece, max(128, BLOCK_BYTES // (2 * inner)))


def add_all(own, *others):
    total = own
    for other in others:
        total = total + other.astype(F32)
    return total


def both_rows(values):
    return values.astype(F32) + swap_x(values).astype(F32)


def solve(
    inverse_quarter,
    inverse_half,
    inverse_root,
    quarter_to_half,
    quarter_to_root,
    half_to_root,
    right_quarter,
    right_half,
    right_root,
    row_flags,
):
    sub_index = lax.axis_index("sub")
    column = lax.axis_index("col")
    low = sub_index % 2
    high = sub_index // 2
    zs = range(4)
    mask_half, mask_root, mask_upper = row_flags[0], row_flags[1], row_flags[2]
    near = [1, 2, 3, 0]
    panel_rows, panel_columns = quarter_to_half.shape
    piece_rows = panel_rows // 2

    col_blocks = listed(*[column ^ d for d in zs])
    col_visit = listed(*[column ^ d for d in near])
    low_visit = listed(low ^ 1, low)
    high_visit = listed(high ^ 1, high)
    low_blocks = listed(low, low ^ 1)
    high_blocks = listed(high, high ^ 1)
    half_blocks = listed(*[(low ^ a) * 4 + (column ^ d) for a in (0, 1) for d in zs])
    half_visit = listed(*[(low ^ a) * 4 + (column ^ d) for a in (1, 0) for d in zs])
    root_visit = listed(
        *[((low ^ a) * 2 + (high ^ b)) * 4 + (column ^ d) for a in (1, 0) for b in (0, 1) for d in zs]
    )
    root_blocks = listed(
        *[((low ^ a) * 2 + (high ^ b)) * 4 + (column ^ d) for a in (0, 1) for b in (0, 1) for d in zs]
    )
    one = jnp.zeros((1,), jnp.int32)

    rows, inner = inverse_quarter.shape
    piece = rows // 4
    tile = tile_of(piece, inner)
    *sends, own = multiply(
        inverse_quarter, [right_quarter], one, spread(col_visit, piece, tile),
        [(piece, BF16)] * 3 + [(piece, F32)],
    )
    quarter_piece = add_all(own, *[swap_z(s, d) for s, d in zip(sends, (1, 2, 3))]).astype(BF16)
    quarter_parts = [quarter_piece] + [swap_z(quarter_piece, d) for d in (1, 2, 3)]

    send, own = multiply(
        quarter_to_half, quarter_parts, col_blocks, spread(low_visit, piece_rows, BLK),
        [(piece_rows, BF16), (piece_rows, F32)], flags=mask_half,
    )
    half_terms = both_rows(add_all(own, swap_core(send)).astype(BF16))
    half_right = (right_half.astype(F32) - half_terms).astype(BF16)
    (root_part,) = multiply(
        quarter_to_root, quarter_parts, col_blocks, spread(high_visit, piece_rows, BLK),
        [(panel_rows, F32)], flags=mask_root,
    )

    rows, inner = inverse_half.shape
    piece = rows // 8
    tile = tile_of(piece, inner)
    send, own = multiply(
        inverse_half, [half_right], one, spread(half_visit, piece, tile),
        [(rows // 2, BF16), (rows // 2, F32)],
    )
    total = add_all(own, swap_core(send))
    sends = [total[d * piece : (d + 1) * piece].astype(BF16) for d in zs]
    half_piece = add_all(total[:piece], *[swap_z(sends[d], d) for d in (1, 2, 3)]).astype(BF16)
    half_parts = [half_piece] + [swap_z(half_piece, d) for d in (1, 2, 3)]
    half_parts = half_parts + [swap_core(p) for p in half_parts]

    send, own = multiply(
        half_to_root, half_parts, half_blocks, spread(high_visit, piece_rows, BLK),
        [(piece_rows, BF16), (piece_rows, F32)], flags=mask_upper, addend=root_part,
    )
    root_terms = both_rows(add_all(own, swap_y(send)).astype(BF16))
    root_right = (right_root.astype(F32) - root_terms).astype(BF16)

    rows, inner = inverse_root.shape
    piece = rows // 16
    tile = tile_of(piece, inner)
    send, own = multiply(
        inverse_root, [root_right], one, spread(root_visit, piece, tile),
        [(rows // 2, BF16), (rows // 2, F32)],
    )
    total = add_all(own, swap_core(send))
    quarter_rows = rows // 4
    totals = []
    for d in zs:
        kept = total[d * piece : (d + 1) * piece]
        sent = total[quarter_rows + d * piece : quarter_rows + (d + 1) * piece]
        totals.append(add_all(kept, swap_y(sent.astype(BF16))))
    root_piece = add_all(
        totals[0], *[swap_z(totals[d].astype(BF16), d) for d in (1, 2, 3)]
    ).astype(BF16)

    root_piece = root_piece.T
    root_parts = [root_piece] + [swap_z(root_piece, d) for d in (1, 2, 3)]
    root_parts = root_parts + [swap_y(p) for p in root_parts]
    root_parts = root_parts + [swap_core(p) for p in root_parts]
    inner, columns = inverse_root.shape
    tile = tile_of(columns, inner)
    (partial,) = multiply_back(
        inverse_root, root_parts, root_blocks, jnp.arange(columns // tile, dtype=jnp.int32),
        [(columns, BF16)],
    )
    root_solution = both_rows(partial).astype(BF16)
    root_pieces = [root_solution, swap_y(root_solution)]

    piece = panel_columns // 8
    tile = tile_of(piece, panel_rows)
    send, own = multiply_back(
        half_to_root, root_pieces, high_blocks, spread(half_visit, piece, tile),
        [(panel_columns // 2, BF16), (panel_columns // 2, F32)], flags=mask_upper,
    )
    total = add_all(own, swap_core(send))
    sends = [total[:, d * piece : (d + 1) * piece].astype(BF16) for d in zs]
    upper_total = add_all(total[:, :piece], *[swap_z(sends[d], d) for d in (1, 2, 3)])
    update = (half_piece.T.astype(F32) - upper_total).astype(BF16)
    update_parts = [update] + [swap_z(update, d) for d in (1, 2, 3)]
    update_parts = update_parts + [swap_core(p) for p in update_parts]
    piece = panel_columns // 4
    tile = tile_of(piece, panel_rows)
    (quarter_back,) = multiply_back(
        quarter_to_root, root_pieces, high_blocks, spread(col_visit, piece, tile),
        [(panel_columns, F32)], flags=mask_root,
    )

    inner, columns = inverse_half.shape
    tile = tile_of(columns, inner)
    (partial,) = multiply_back(
        inverse_half, update_parts, half_blocks, jnp.arange(columns // tile, dtype=jnp.int32),
        [(columns, BF16)],
    )
    half_solution = both_rows(partial).astype(BF16)
    half_pieces = [half_solution, swap_core(half_solution)]

    tile = tile_of(piece, panel_rows)
    *sends, own = multiply_back(
        quarter_to_half, half_pieces, low_blocks, spread(col_visit, piece, tile),
        [(piece, BF16)] * 3 + [(piece, F32)], flags=mask_half, addend=quarter_back,
    )
    quarter_total = add_all(own, *[swap_z(s, d) for s, d in zip(sends, (1, 2, 3))])
    update = (quarter_piece.T.astype(F32) - quarter_total).astype(BF16)
    update_parts = [update] + [swap_z(update, d) for d in (1, 2, 3)]
    inner, columns = inverse_quarter.shape
    tile = tile_of(columns, inner)
    own, send = multiply_back(
        inverse_quarter, update_parts, col_blocks, jnp.arange(columns // tile, dtype=jnp.int32),
        [], side=lax.axis_index("row"),
    )
    return own + swap_x(send).astype(F32), half_solution.T, root_solution.T


def pick(values, index):
    return lax.dynamic_index_in_dim(values, index, 0, keepdims=False)


def is_power_of_two(count):
    return count & (count - 1) == 0


def scatter_sum(partial, axis):
    count = lax.axis_size(axis)
    own = lax.axis_index(axis)
    pieces = partial.reshape(count, partial.shape[0] // count, partial.shape[1])
    total = pick(pieces, own)
    for distance in range(1, count):
        total = total + swap(pick(pieces, own ^ distance).astype(BF16), axis, distance).astype(F32)
    return total


def gather(piece, axis):
    count = lax.axis_size(axis)
    own = lax.axis_index(axis)
    whole = jnp.zeros((count,) + piece.shape, piece.dtype)
    whole = lax.dynamic_update_index_in_dim(whole, piece, own, 0)
    for distance in range(1, count):
        whole = lax.dynamic_update_index_in_dim(
            whole, swap(piece, axis, distance), own ^ distance, 0
        )
    return whole.reshape((count * piece.shape[0],) + piece.shape[1:])


def pair_scatter(halves, bit_value, axis, distance):
    own_piece = pick(halves, bit_value)
    other_piece = pick(halves, 1 - bit_value)
    return own_piece + swap(other_piece.astype(BF16), axis, distance).astype(F32)


def pair_gather(piece, bit_value, axis, distance):
    other = swap(piece, axis, distance)
    return jnp.where(bit_value == 0, jnp.stack([piece, other]), jnp.stack([other, piece]))


def sum_rows(values):
    if lax.axis_size("row") != 2:
        return lax.psum(values, "row")
    sent = values.astype(BF16)
    return sent.astype(F32) + swap(sent, "row", 1).astype(F32)


def project(matrix, vector):
    halves, height, inner = matrix.shape
    flat = jnp.dot(
        matrix.reshape(halves * height, inner), vector, preferred_element_type=F32
    )
    return flat.reshape(halves, height, vector.shape[1])


def transposed(matrix, vector):
    return lax.dot_general(
        matrix, vector, (((0,), (0,)), ((), ())), preferred_element_type=F32
    )


def project_back(matrix, pieces):
    return transposed(
        matrix.reshape(-1, matrix.shape[2]), pieces.reshape(-1, pieces.shape[2])
    )


def halve(values):
    return values.reshape(2, values.shape[0] // 2, values.shape[1])


def join(values):
    return values.reshape(-1, values.shape[2])


def final_sum(values):
    if lax.axis_size("row") != 2:
        return lax.psum_scatter(values, "row", scatter_dimension=1, tiled=True)
    own = lax.axis_index("row")
    width = values.shape[1] // 2
    mine = lax.dynamic_slice_in_dim(values, own * width, width, 1)
    sent = lax.dynamic_slice_in_dim(values, (1 - own) * width, width, 1)
    return mine + swap(sent.astype(BF16), "row", 1).astype(F32)


def solve_plain(
    inverse_quarter,
    inverse_half,
    inverse_root,
    quarter_to_half,
    quarter_to_root,
    half_to_root,
    right_quarter,
    right_half,
    right_root,
    masking,
):
    sub_index = lax.axis_index("sub")
    low_bit = sub_index % 2
    high_bit = sub_index // 2
    mask_half, mask_root, mask_upper = masking[0], masking[1], masking[2]

    quarter_partial = jnp.dot(inverse_quarter, right_quarter, preferred_element_type=F32)
    quarter_piece = scatter_sum(quarter_partial, "col").astype(BF16)
    solved_quarter = gather(quarter_piece, "col")

    half_part = project(quarter_to_half, solved_quarter) * mask_half
    half_terms = sum_rows(pair_scatter(half_part, low_bit, "sub", 1))
    half_right = (right_half.astype(F32) - half_terms).astype(BF16)
    root_part = project(quarter_to_root, solved_quarter) * mask_root

    half_partial = jnp.dot(inverse_half, half_right, preferred_element_type=F32)
    half_partial = pair_scatter(halve(half_partial), low_bit, "sub", 1)
    half_piece = scatter_sum(half_partial, "col").astype(BF16)
    solved_half = join(pair_gather(gather(half_piece, "col"), low_bit, "sub", 1))

    upper_part = project(half_to_root, solved_half) * mask_upper
    root_terms = sum_rows(pair_scatter(upper_part + root_part, high_bit, "sub", 2))
    root_right = (right_root.astype(F32) - root_terms).astype(BF16)

    root_partial = jnp.dot(inverse_root, root_right, preferred_element_type=F32)
    root_partial = pair_scatter(halve(root_partial), low_bit, "sub", 1)
    root_partial = pair_scatter(halve(root_partial), high_bit, "sub", 2)
    root_piece = scatter_sum(root_partial, "col").astype(BF16)
    solved_root = join(pair_gather(gather(root_piece, "col"), high_bit, "sub", 2))
    solved_root = join(pair_gather(solved_root, low_bit, "sub", 1))

    root_solution = sum_rows(transposed(inverse_root, solved_root)).astype(BF16)
    root_pieces = pair_gather(root_solution, high_bit, "sub", 2)

    upper_back = project_back(half_to_root, root_pieces * mask_upper.astype(BF16))
    upper_back = pair_scatter(halve(upper_back), low_bit, "sub", 1)
    upper_total = scatter_sum(upper_back, "col")
    half_update_piece = (half_piece.astype(F32) - upper_total).astype(BF16)
    half_update = join(pair_gather(gather(half_update_piece, "col"), low_bit, "sub", 1))
    quarter_back = project_back(quarter_to_root, root_pieces * mask_root.astype(BF16))

    half_solution = sum_rows(transposed(inverse_half, half_update)).astype(BF16)
    half_pieces = pair_gather(half_solution, low_bit, "sub", 1)

    quarter_back = quarter_back + project_back(
        quarter_to_half, half_pieces * mask_half.astype(BF16)
    )
    quarter_total = scatter_sum(quarter_back, "col")
    quarter_update_piece = (quarter_piece.astype(F32) - quarter_total).astype(BF16)
    quarter_update = gather(quarter_update_piece, "col")
    return transposed(inverse_quarter, quarter_update), half_solution, root_solution


def per_device(
    inverse_quarter,
    inverse_half,
    inverse_root,
    quarter_to_half,
    quarter_to_root,
    half_to_root,
    right_quarter,
    right_half,
    right_root,
    row_blocks,
):
    sub_index = lax.axis_index("sub")
    column_index = lax.axis_index("col")
    block_count = quarter_to_half.shape[2] // BLK
    row_flags = lax.dynamic_slice(
        row_blocks,
        (jnp.int32(0), sub_index, jnp.int32(0), column_index * block_count),
        (3, 1, 2, block_count),
    )[:, 0]
    smallest = min(inverse_quarter.shape[1] // 4, inverse_half.shape[1] // 8, inverse_root.shape[0] // 16)
    if (lax.axis_size("row"), lax.axis_size("col")) != (2, 4) or smallest % 128:
        quarter, half, root = solve_plain(
            inverse_quarter[0],
            inverse_half[0],
            inverse_root,
            quarter_to_half[0],
            quarter_to_root[0],
            half_to_root[0],
            right_quarter[0],
            right_half[0],
            right_root,
            jnp.repeat(row_flags, BLK, axis=2).astype(F32)[:, :, :, None],
        )
        return (final_sum(quarter)[None], half[None], root)
    panels = [p[0].reshape(-1, p.shape[3]) for p in (quarter_to_half, quarter_to_root, half_to_root)]
    quarter, half, root = solve(
        inverse_quarter[0],
        inverse_half[0],
        inverse_root,
        *panels,
        right_quarter[0],
        right_half[0],
        right_root,
        row_flags.reshape(3, -1),
    )
    return (quarter[None], half[None], root)


def solution(mesh):
    placed = (
        P("sub", "row", "col"),
        P("sub", "row", "col"),
        P("row", ("sub", "col")),
        P("sub", None, "col", "row"),
        P("sub", None, "col", "row"),
        P("sub", None, "col", "row"),
        P("sub", "col", None),
        P("sub", "col", None),
        P(("sub", "col"), None),
        P(),
    )
    return jax.shard_map(
        per_device,
        mesh=mesh,
        in_specs=placed,
        out_specs=(P("sub", "col", "row"), P("sub", "col", None), P(("sub", "col"), None)),
        check_vma=False,
    )
```

```python
import jax
import jax.numpy as jnp
from jax import lax
from jax.experimental import pallas as pl
from jax.experimental.pallas import tpu as pltpu
from jax.sharding import PartitionSpec as P

BLK = 256
STREAMS = 2
KERNEL_VMEM = 20 << 20
F32 = jnp.float32
BF16 = jnp.bfloat16


def swap(values, axis, distance):
    pairs = [(i, i ^ distance) for i in range(lax.axis_size(axis))]
    return lax.ppermute(values, axis, pairs)


def swap_core(values):
    return swap(values, "sub", 1)


def swap_y(values):
    return swap(values, "sub", 2)


def swap_z(values, distance):
    return swap(values, "col", distance)


def swap_x(values):
    return swap(values, "row", 1)


def fetch(matrix, after=None):
    def body(*refs):
        copy = pltpu.make_async_copy(refs[0], refs[-2], refs[-1])
        copy.start()
        copy.wait()

    matrix = pltpu.with_memory_space_constraint(matrix, pltpu.HBM)
    operands = [matrix] if after is None else [matrix, after]
    return pl.pallas_call(
        body,
        in_specs=[pl.BlockSpec(memory_space=pltpu.HBM)] * len(operands),
        out_specs=pl.BlockSpec(memory_space=pltpu.VMEM),
        out_shape=jax.ShapeDtypeStruct(matrix.shape, matrix.dtype),
        scratch_shapes=[pltpu.SemaphoreType.DMA],
        compiler_params=pltpu.CompilerParams(vmem_limit_bytes=1 << 20),
        cost_estimate=pl.CostEstimate(
            flops=0, transcendentals=0, bytes_accessed=4 * matrix.size
        ),
        name="fetch",
    )(*operands)


def multiply(matrix, vectors, in_blocks, order, outs, flags=None, addend=None):
    rows, inner = matrix.shape
    width = vectors[0].shape[1]
    steps = order.shape[0]
    tile = rows // steps
    in_size = inner // in_blocks.shape[0]
    starts = [0]
    for out_rows, _ in outs:
        starts.append(starts[-1] + out_rows // tile)
    count = len(vectors)
    gathered = count > 1

    def body(places, visit, shown, *refs):
        vector_refs = refs[:count]
        matrix_ref = refs[count]
        addend_ref = refs[count + 1] if addend is not None else None
        out_refs = refs[count + 1 + (addend is not None) :][: len(outs)]
        step = pl.program_id(0)
        if gathered:
            x_ref = refs[-1]

            @pl.when(step == 0)
            def _():
                at = 0
                for ref in vector_refs:
                    for part in range(ref.shape[0] // in_size):
                        place = pl.multiple_of(places[at] * in_size, in_size)
                        x_ref[pl.ds(place, in_size), :] = ref[part * in_size : (part + 1) * in_size, :]
                        at += 1

        else:
            x_ref = vector_refs[0]
        first_row = pl.multiple_of(visit[step] * tile, tile)
        total = jnp.dot(
            matrix_ref[pl.ds(first_row, tile), :], x_ref[...], preferred_element_type=F32
        )
        if flags is not None:
            block = visit[step] * (tile // BLK)
            total = jnp.concatenate(
                [
                    total[i * BLK : (i + 1) * BLK] * shown[block + i].astype(F32)
                    for i in range(tile // BLK)
                ]
            )
        if addend is not None:
            total = total + addend_ref[...]
        for index, ref in enumerate(out_refs):

            @pl.when((step >= starts[index]) & (step < starts[index + 1]))
            def _():
                ref[...] = total.astype(ref.dtype)

    def out_map(first, last):
        return lambda i, *_: (jnp.clip(i - first, 0, last - first - 1), 0)

    in_specs = [pl.BlockSpec(memory_space=pltpu.VMEM)] * (count + 1)
    operands = list(vectors) + [matrix]
    if addend is not None:
        in_specs.append(pl.BlockSpec((tile, width), lambda i, *_: (i, 0)))
        operands.append(addend)
    return pl.pallas_call(
        body,
        grid_spec=pltpu.PrefetchScalarGridSpec(
            num_scalar_prefetch=3,
            grid=(steps,),
            in_specs=in_specs,
            out_specs=[
                pl.BlockSpec((tile, width), out_map(starts[i], starts[i + 1]))
                for i in range(len(outs))
            ],
            scratch_shapes=[pltpu.VMEM((inner, width), BF16)] if gathered else [],
        ),
        out_shape=[jax.ShapeDtypeStruct((r, width), t) for r, t in outs],
        compiler_params=pltpu.CompilerParams(vmem_limit_bytes=KERNEL_VMEM),
        cost_estimate=pl.CostEstimate(
            flops=2 * rows * inner * width,
            transcendentals=0,
            bytes_accessed=4 * (rows + inner) * width,
        ),
        name="multiply",
    )(in_blocks, order, jnp.zeros((1,), jnp.int32) if flags is None else flags, *operands)


def multiply_back(matrix, vectors, in_blocks, order, outs, flags=None, addend=None):
    inner, columns = matrix.shape
    width = vectors[0].shape[0]
    steps = order.shape[0]
    tile = columns // steps
    in_size = inner // in_blocks.shape[0]
    mask_size = min(BLK, in_size)
    starts = [0]
    for out_columns, _ in outs:
        starts.append(starts[-1] + out_columns // tile)
    count = len(vectors)

    def body(places, visit, shown, *refs):
        vector_refs = refs[:count]
        matrix_ref = refs[count]
        addend_ref = refs[count + 1] if addend is not None else None
        y_ref = refs[-1]
        out_refs = refs[count + 1 + (addend is not None) : -1]
        step = pl.program_id(0)

        @pl.when(step == 0)
        def _():
            at = 0
            for ref in vector_refs:
                for part in range(ref.shape[1] // in_size):
                    if flags is None:
                        place = pl.multiple_of(places[at] * in_size, in_size)
                        y_ref[:, pl.ds(place, in_size)] = ref[:, part * in_size : (part + 1) * in_size]
                    else:
                        for inside in range(in_size // mask_size):
                            block = places[at] * (in_size // mask_size) + inside
                            place = pl.multiple_of(block * mask_size, mask_size)
                            start = part * in_size + inside * mask_size
                            held = ref[:, start : start + mask_size]
                            y_ref[:, pl.ds(place, mask_size)] = jnp.where(
                                shown[block] != 0, held, jnp.zeros_like(held)
                            )
                    at += 1

        first_column = pl.multiple_of(visit[step] * tile, tile)
        total = jnp.dot(
            y_ref[...], matrix_ref[:, pl.ds(first_column, tile)], preferred_element_type=F32
        )
        if addend is not None:
            total = total + addend_ref[...]
        for index, ref in enumerate(out_refs):

            @pl.when((step >= starts[index]) & (step < starts[index + 1]))
            def _():
                ref[...] = total.astype(ref.dtype)

    def out_map(first, last):
        return lambda i, *_: (0, jnp.clip(i - first, 0, last - first - 1))

    in_specs = [pl.BlockSpec(memory_space=pltpu.VMEM)] * (count + 1)
    operands = list(vectors) + [matrix]
    if addend is not None:
        in_specs.append(pl.BlockSpec((width, tile), lambda i, *_: (0, i)))
        operands.append(addend)
    return pl.pallas_call(
        body,
        grid_spec=pltpu.PrefetchScalarGridSpec(
            num_scalar_prefetch=3,
            grid=(steps,),
            in_specs=in_specs,
            out_specs=[
                pl.BlockSpec((width, tile), out_map(starts[i], starts[i + 1]))
                for i in range(len(outs))
            ],
            scratch_shapes=[pltpu.VMEM((width, inner), BF16)],
        ),
        out_shape=[jax.ShapeDtypeStruct((width, c), t) for c, t in outs],
        compiler_params=pltpu.CompilerParams(vmem_limit_bytes=KERNEL_VMEM),
        cost_estimate=pl.CostEstimate(
            flops=2 * columns * inner * width,
            transcendentals=0,
            bytes_accessed=4 * (columns + inner) * width,
        ),
        name="multiply_back",
    )(in_blocks, order, jnp.zeros((1,), jnp.int32) if flags is None else flags, *operands)


def flip(values):
    def body(in_ref, out_ref):
        out_ref[...] = in_ref[...].T

    rows, columns = values.shape
    tile = min(rows, 256)
    return pl.pallas_call(
        body,
        grid=(rows // tile,),
        in_specs=[pl.BlockSpec((tile, columns), lambda i: (i, 0))],
        out_specs=pl.BlockSpec((columns, tile), lambda i: (0, i)),
        out_shape=jax.ShapeDtypeStruct((columns, rows), values.dtype),
        name="flip",
    )(values)


def listed(*values):
    return jnp.stack([jnp.asarray(v, jnp.int32) for v in values])


def spread(blocks, size, tile):
    parts = size // tile
    return (blocks[:, None] * parts + jnp.arange(parts, dtype=jnp.int32)[None]).reshape(-1)


def add_all(own, *others):
    total = own
    for other in others:
        total = total + other.astype(F32)
    return total


def both_rows(values):
    return values.astype(F32) + swap_x(values).astype(F32)


def reduce_z(far_send, near_send, far_own, own):
    passed = add_all(far_own, swap_z(far_send, 1)).astype(BF16)
    return add_all(own, swap_z(near_send, 1), swap_z(passed, 3))


def gather_z(piece):
    across = swap_z(piece, 3)
    beside = swap_z(piece, 1)
    return [piece, beside, swap_z(across, 1), across]


def cut(values, count, axis):
    size = values.shape[axis] // count
    return [lax.slice_in_dim(values, i * size, (i + 1) * size, axis=axis) for i in range(count)]


def paired(parts, axis):
    return [jnp.concatenate(parts[:2], axis=axis), jnp.concatenate(parts[2:], axis=axis)]


def reduce_core_z(send, own, axis):
    total = add_all(own, swap_core(send))
    far_send, near_send, far_own, own = cut(total, 4, axis)
    return reduce_z(far_send.astype(BF16), near_send.astype(BF16), far_own, own)


def reduce_core_y_z(send, own, axis):
    kept, sent = cut(add_all(own, swap_core(send)), 2, axis)
    passed, final = [
        add_all(k, swap_y(s.astype(BF16))) for k, s in zip(cut(kept, 2, axis), cut(sent, 2, axis))
    ]
    far_send, near_send = cut(passed, 2, axis)
    far_own, own = cut(final, 2, axis)
    return reduce_z(far_send.astype(BF16), near_send.astype(BF16), far_own, own)


def gather_z_core(piece, axis):
    parts = paired(gather_z(piece), axis)
    return parts + [swap_core(p) for p in parts]


def gather_z_y_core(piece, axis):
    parts = paired(gather_z(piece), axis)
    parts = parts + [swap_y(p) for p in parts]
    return parts + [swap_core(p) for p in parts]


def solve(
    inverse_quarter,
    inverse_half,
    inverse_root,
    quarter_to_half,
    quarter_to_root,
    half_to_root,
    right_quarter,
    right_half,
    right_root,
    row_flags,
):
    sub_index = lax.axis_index("sub")
    column = lax.axis_index("col")
    low = sub_index % 2
    high = sub_index // 2
    zs = range(4)
    visit_z = (2, 1, 3, 0)
    mask_half, mask_root, mask_upper = row_flags[0], row_flags[1], row_flags[2]
    panel_rows, panel_columns = quarter_to_half.shape
    piece_rows = panel_rows // 2
    panel_tile = min(piece_rows, 1024)

    col_blocks = listed(*[column ^ d for d in zs])
    col_visit = listed(*[column ^ d for d in visit_z])
    low_blocks = listed(low, low ^ 1)
    high_blocks = listed(high, high ^ 1)
    low_visit = spread(listed(low ^ 1, low), piece_rows, panel_tile)
    high_visit = spread(listed(high ^ 1, high), piece_rows, panel_tile)
    half_blocks = listed(*[(low ^ a) * 4 + (column ^ d) for a in (0, 1) for d in zs])
    half_visit = listed(*[(low ^ a) * 4 + (column ^ d) for a in (1, 0) for d in visit_z])
    root_place = lambda a, b, d: ((low ^ a) * 2 + (high ^ b)) * 4 + (column ^ d)
    root_visit = listed(*[root_place(a, b, d) for a in (1, 0) for b in (0, 1) for d in visit_z])
    root_blocks = listed(*[root_place(a, b, d) for a in (0, 1) for b in (0, 1) for d in zs])
    one = jnp.zeros((1,), jnp.int32)
    in_turn = lambda columns: jnp.arange(columns // min(columns, 512), dtype=jnp.int32)

    rows = inverse_quarter.shape[0]
    held = fetch(inverse_quarter)
    parts = [
        multiply(
            held, [x], one, col_visit, [(rows // 4, BF16)] * 2 + [(rows // 4, F32)] * 2
        )
        for x in right_quarter
    ]
    quarter_piece = [reduce_z(*p).astype(BF16) for p in parts]
    held = fetch(quarter_to_half, quarter_piece[0])
    quarter_parts = [gather_z(p) for p in quarter_piece]

    parts = [
        multiply(
            held, x, col_blocks, low_visit, [(piece_rows, BF16), (piece_rows, F32)], flags=mask_half
        )
        for x in quarter_parts
    ]
    held_root = fetch(quarter_to_root, parts[0][0])
    half_right = [
        (r.astype(F32) - both_rows(add_all(own, swap_core(send)).astype(BF16))).astype(BF16)
        for r, (send, own) in zip(right_half, parts)
    ]
    root_part = [
        multiply(held_root, x, col_blocks, high_visit, [(panel_rows, F32)], flags=mask_root)[0]
        for x in quarter_parts
    ]

    held = fetch(inverse_half, root_part[0])
    rows = inverse_half.shape[0]
    parts = [
        multiply(held, [x], one, half_visit, [(rows // 2, BF16), (rows // 2, F32)])
        for x in half_right
    ]
    half_piece = [reduce_core_z(send, own, 0).astype(BF16) for send, own in parts]
    held = fetch(half_to_root, half_piece[0])
    half_parts = [gather_z_core(p, 0) for p in half_piece]

    parts = [
        multiply(
            held, x, half_blocks, high_visit, [(piece_rows, BF16), (piece_rows, F32)],
            flags=mask_upper, addend=early,
        )
        for x, early in zip(half_parts, root_part)
    ]
    held_root = fetch(inverse_root, parts[0][0])
    root_right = [
        (r.astype(F32) - both_rows(add_all(own, swap_y(send)).astype(BF16))).astype(BF16)
        for r, (send, own) in zip(right_root, parts)
    ]

    rows = inverse_root.shape[0]
    parts = [
        multiply(held_root, [x], one, root_visit, [(rows // 2, BF16), (rows // 2, F32)])
        for x in root_right
    ]

    root_piece = [flip(reduce_core_y_z(send, own, 0).astype(BF16)) for send, own in parts]
    held_root = fetch(inverse_root, root_piece[0])
    root_parts = [gather_z_y_core(p, 1) for p in root_piece]
    columns = inverse_root.shape[1]
    parts = [
        multiply_back(held_root, y, root_blocks, in_turn(columns), [(columns, BF16)])[0]
        for y in root_parts
    ]
    held = fetch(half_to_root, parts[0])
    root_solution = [both_rows(p).astype(BF16) for p in parts]
    root_pieces = [[p, swap_y(p)] for p in root_solution]

    parts = [
        multiply_back(
            held, y, high_blocks, half_visit,
            [(panel_columns // 2, BF16), (panel_columns // 2, F32)], flags=mask_upper,
        )
        for y in root_pieces
    ]
    held_root = fetch(quarter_to_root, parts[0][0])
    update = [
        (flip(p).astype(F32) - reduce_core_z(send, own, 1)).astype(BF16)
        for p, (send, own) in zip(half_piece, parts)
    ]
    update_parts = [gather_z_core(p, 1) for p in update]
    quarter_back = [
        multiply_back(held_root, y, high_blocks, col_visit, [(panel_columns, F32)], flags=mask_root)[0]
        for y in root_pieces
    ]

    columns = inverse_half.shape[1]
    held = fetch(inverse_half, quarter_back[0])
    parts = [
        multiply_back(held, y, half_blocks, in_turn(columns), [(columns, BF16)])[0]
        for y in update_parts
    ]
    held_root = fetch(quarter_to_half, parts[0])
    half_solution = [both_rows(p).astype(BF16) for p in parts]
    half_pieces = [[p, swap_core(p)] for p in half_solution]

    piece = panel_columns // 4
    parts = [
        multiply_back(
            held_root, y, low_blocks, col_visit, [(piece, BF16)] * 2 + [(piece, F32)] * 2,
            flags=mask_half, addend=early,
        )
        for y, early in zip(half_pieces, quarter_back)
    ]
    update = [
        (flip(q).astype(F32) - reduce_z(*p)).astype(BF16) for q, p in zip(quarter_piece, parts)
    ]
    held = fetch(inverse_quarter, update[0])
    columns = inverse_quarter.shape[1]
    quarter = [
        multiply_back(held, gather_z(y), col_blocks, in_turn(columns), [(columns, F32)])[0]
        for y in update
    ]
    return quarter, [flip(p) for p in half_solution], [flip(p) for p in root_solution]


def pick(values, index):
    return lax.dynamic_index_in_dim(values, index, 0, keepdims=False)


def is_power_of_two(count):
    return count & (count - 1) == 0


def scatter_sum(partial, axis):
    count = lax.axis_size(axis)
    own = lax.axis_index(axis)
    pieces = partial.reshape(count, partial.shape[0] // count, partial.shape[1])
    total = pick(pieces, own)
    for distance in range(1, count):
        total = total + swap(pick(pieces, own ^ distance).astype(BF16), axis, distance).astype(F32)
    return total


def gather(piece, axis):
    count = lax.axis_size(axis)
    own = lax.axis_index(axis)
    whole = jnp.zeros((count,) + piece.shape, piece.dtype)
    whole = lax.dynamic_update_index_in_dim(whole, piece, own, 0)
    for distance in range(1, count):
        whole = lax.dynamic_update_index_in_dim(
            whole, swap(piece, axis, distance), own ^ distance, 0
        )
    return whole.reshape((count * piece.shape[0],) + piece.shape[1:])


def pair_scatter(halves, bit_value, axis, distance):
    own_piece = pick(halves, bit_value)
    other_piece = pick(halves, 1 - bit_value)
    return own_piece + swap(other_piece.astype(BF16), axis, distance).astype(F32)


def pair_gather(piece, bit_value, axis, distance):
    other = swap(piece, axis, distance)
    return jnp.where(bit_value == 0, jnp.stack([piece, other]), jnp.stack([other, piece]))


def sum_rows(values):
    if lax.axis_size("row") != 2:
        return lax.psum(values, "row")
    sent = values.astype(BF16)
    return sent.astype(F32) + swap(sent, "row", 1).astype(F32)


def project(matrix, vector):
    halves, height, inner = matrix.shape
    flat = jnp.dot(
        matrix.reshape(halves * height, inner), vector, preferred_element_type=F32
    )
    return flat.reshape(halves, height, vector.shape[1])


def transposed(matrix, vector):
    return lax.dot_general(
        matrix, vector, (((0,), (0,)), ((), ())), preferred_element_type=F32
    )


def project_back(matrix, pieces):
    return transposed(
        matrix.reshape(-1, matrix.shape[2]), pieces.reshape(-1, pieces.shape[2])
    )


def halve(values):
    return values.reshape(2, values.shape[0] // 2, values.shape[1])


def join(values):
    return values.reshape(-1, values.shape[2])


def final_sum(values):
    if lax.axis_size("row") != 2:
        return lax.psum_scatter(values, "row", scatter_dimension=1, tiled=True)
    own = lax.axis_index("row")
    width = values.shape[1] // 2
    mine = lax.dynamic_slice_in_dim(values, own * width, width, 1)
    sent = lax.dynamic_slice_in_dim(values, (1 - own) * width, width, 1)
    return mine + swap(sent.astype(BF16), "row", 1).astype(F32)


def solve_plain(
    inverse_quarter,
    inverse_half,
    inverse_root,
    quarter_to_half,
    quarter_to_root,
    half_to_root,
    right_quarter,
    right_half,
    right_root,
    masking,
):
    sub_index = lax.axis_index("sub")
    low_bit = sub_index % 2
    high_bit = sub_index // 2
    mask_half, mask_root, mask_upper = masking[0], masking[1], masking[2]

    quarter_partial = jnp.dot(inverse_quarter, right_quarter, preferred_element_type=F32)
    quarter_piece = scatter_sum(quarter_partial, "col").astype(BF16)
    solved_quarter = gather(quarter_piece, "col")

    half_part = project(quarter_to_half, solved_quarter) * mask_half
    half_terms = sum_rows(pair_scatter(half_part, low_bit, "sub", 1))
    half_right = (right_half.astype(F32) - half_terms).astype(BF16)
    root_part = project(quarter_to_root, solved_quarter) * mask_root

    half_partial = jnp.dot(inverse_half, half_right, preferred_element_type=F32)
    half_partial = pair_scatter(halve(half_partial), low_bit, "sub", 1)
    half_piece = scatter_sum(half_partial, "col").astype(BF16)
    solved_half = join(pair_gather(gather(half_piece, "col"), low_bit, "sub", 1))

    upper_part = project(half_to_root, solved_half) * mask_upper
    root_terms = sum_rows(pair_scatter(upper_part + root_part, high_bit, "sub", 2))
    root_right = (right_root.astype(F32) - root_terms).astype(BF16)

    root_partial = jnp.dot(inverse_root, root_right, preferred_element_type=F32)
    root_partial = pair_scatter(halve(root_partial), low_bit, "sub", 1)
    root_partial = pair_scatter(halve(root_partial), high_bit, "sub", 2)
    root_piece = scatter_sum(root_partial, "col").astype(BF16)
    solved_root = join(pair_gather(gather(root_piece, "col"), high_bit, "sub", 2))
    solved_root = join(pair_gather(solved_root, low_bit, "sub", 1))

    root_solution = sum_rows(transposed(inverse_root, solved_root)).astype(BF16)
    root_pieces = pair_gather(root_solution, high_bit, "sub", 2)

    upper_back = project_back(half_to_root, root_pieces * mask_upper.astype(BF16))
    upper_back = pair_scatter(halve(upper_back), low_bit, "sub", 1)
    upper_total = scatter_sum(upper_back, "col")
    half_update_piece = (half_piece.astype(F32) - upper_total).astype(BF16)
    half_update = join(pair_gather(gather(half_update_piece, "col"), low_bit, "sub", 1))
    quarter_back = project_back(quarter_to_root, root_pieces * mask_root.astype(BF16))

    half_solution = sum_rows(transposed(inverse_half, half_update)).astype(BF16)
    half_pieces = pair_gather(half_solution, low_bit, "sub", 1)

    quarter_back = quarter_back + project_back(
        quarter_to_half, half_pieces * mask_half.astype(BF16)
    )
    quarter_total = scatter_sum(quarter_back, "col")
    quarter_update_piece = (quarter_piece.astype(F32) - quarter_total).astype(BF16)
    quarter_update = gather(quarter_update_piece, "col")
    return transposed(inverse_quarter, quarter_update), half_solution, root_solution


def per_device(
    inverse_quarter,
    inverse_half,
    inverse_root,
    quarter_to_half,
    quarter_to_root,
    half_to_root,
    right_quarter,
    right_half,
    right_root,
    row_blocks,
):
    sub_index = lax.axis_index("sub")
    column_index = lax.axis_index("col")
    block_count = quarter_to_half.shape[2] // BLK
    row_flags = lax.dynamic_slice(
        row_blocks,
        (jnp.int32(0), sub_index, jnp.int32(0), column_index * block_count),
        (3, 1, 2, block_count),
    )[:, 0]
    smallest = min(inverse_quarter.shape[1] // 4, inverse_half.shape[1] // 8, inverse_root.shape[0] // 16)
    if (lax.axis_size("row"), lax.axis_size("col")) != (2, 4) or smallest % 128:
        quarter, half, root = solve_plain(
            inverse_quarter[0],
            inverse_half[0],
            inverse_root,
            quarter_to_half[0],
            quarter_to_root[0],
            half_to_root[0],
            right_quarter[0],
            right_half[0],
            right_root,
            jnp.repeat(row_flags, BLK, axis=2).astype(F32)[:, :, :, None],
        )
        return (final_sum(quarter)[None], half[None], root)
    panels = [p[0].reshape(-1, p.shape[3]) for p in (quarter_to_half, quarter_to_root, half_to_root)]
    quarter, half, root = solve(
        inverse_quarter[0],
        inverse_half[0],
        inverse_root,
        *panels,
        jnp.split(right_quarter[0], STREAMS, axis=1),
        jnp.split(right_half[0], STREAMS, axis=1),
        jnp.split(right_root, STREAMS, axis=1),
        row_flags.reshape(3, -1),
    )
    low_side, high_side = jnp.split(quarter[0], 2) if STREAMS == 1 else quarter
    first = lax.axis_index("row") == 0
    own = jnp.where(first, low_side, high_side)
    send = jnp.where(first, high_side, low_side).astype(BF16)
    quarter = (own + swap_x(send).astype(F32)).T
    return (quarter[None], jnp.concatenate(half, axis=1)[None], jnp.concatenate(root, axis=1))


def solution(mesh):
    placed = (
        P("sub", "row", "col"),
        P("sub", "row", "col"),
        P("row", ("sub", "col")),
        P("sub", None, "col", "row"),
        P("sub", None, "col", "row"),
        P("sub", None, "col", "row"),
        P("sub", "col", None),
        P("sub", "col", None),
        P(("sub", "col"), None),
        P(),
    )
    return jax.shard_map(
        per_device,
        mesh=mesh,
        in_specs=placed,
        out_specs=(P("sub", "col", "row"), P("sub", "col", None), P(("sub", "col"), None)),
        check_vma=False,
    )
```

```python
import jax
import jax.numpy as jnp
from jax import lax
from jax.experimental import pallas as pl
from jax.experimental.pallas import tpu as pltpu
from jax.sharding import PartitionSpec as P

BLK = 256
STREAMS = 2
KERNEL_VMEM = 20 << 20
F32 = jnp.float32
BF16 = jnp.bfloat16


def swap(values, axis, distance):
    pairs = [(i, i ^ distance) for i in range(lax.axis_size(axis))]
    return lax.ppermute(values, axis, pairs)


def swap_core(values):
    return swap(values, "sub", 1)


def swap_y(values):
    return swap(values, "sub", 2)


def swap_z(values, distance):
    return swap(values, "col", distance)


def swap_x(values):
    return swap(values, "row", 1)


def fetch(matrix, *after, pieces=None, size=None):
    count = 1 if pieces is None else pieces.shape[0]
    rows = matrix.shape[0] if pieces is None else count * size

    def body(*refs):
        source, target, sems = refs[1], refs[-2], refs[-1]
        if pieces is None:
            copies = [pltpu.make_async_copy(source, target, sems.at[0])]
        else:
            copies = [
                pltpu.make_async_copy(
                    source.at[pl.ds(pl.multiple_of(refs[0][i] * size, size), size), :],
                    target.at[pl.ds(i * size, size), :],
                    sems.at[i],
                )
                for i in range(count)
            ]
        for copy in copies:
            copy.start()
        for copy in copies:
            copy.wait()

    operands = [pltpu.with_memory_space_constraint(matrix, pltpu.HBM), *after]
    return pl.pallas_call(
        body,
        grid_spec=pltpu.PrefetchScalarGridSpec(
            num_scalar_prefetch=1,
            grid=(1,),
            in_specs=[pl.BlockSpec(memory_space=pltpu.HBM)] * len(operands),
            out_specs=pl.BlockSpec(memory_space=pltpu.VMEM),
            scratch_shapes=[pltpu.SemaphoreType.DMA((count,))],
        ),
        out_shape=jax.ShapeDtypeStruct((rows, matrix.shape[1]), matrix.dtype),
        compiler_params=pltpu.CompilerParams(vmem_limit_bytes=1 << 20),
        cost_estimate=pl.CostEstimate(
            flops=0, transcendentals=0, bytes_accessed=4 * rows * matrix.shape[1]
        ),
        name="fetch",
    )(jnp.zeros((1,), jnp.int32) if pieces is None else pieces, *operands)


def multiply(matrix, vectors, in_blocks, order, outs, flags=None, addend=None):
    rows, inner = matrix.shape
    width = vectors[0].shape[1]
    steps = order.shape[0]
    tile = rows // steps
    in_size = inner // in_blocks.shape[0]
    starts = [0]
    for out_rows, _ in outs:
        starts.append(starts[-1] + out_rows // tile)
    count = len(vectors)
    gathered = count > 1

    def body(places, visit, shown, *refs):
        vector_refs = refs[:count]
        matrix_ref = refs[count]
        addend_ref = refs[count + 1] if addend is not None else None
        out_refs = refs[count + 1 + (addend is not None) :][: len(outs)]
        step = pl.program_id(0)
        if gathered:
            x_ref = refs[-1]

            @pl.when(step == 0)
            def _():
                at = 0
                for ref in vector_refs:
                    for part in range(ref.shape[0] // in_size):
                        place = pl.multiple_of(places[at] * in_size, in_size)
                        x_ref[pl.ds(place, in_size), :] = ref[part * in_size : (part + 1) * in_size, :]
                        at += 1

        else:
            x_ref = vector_refs[0]
        first_row = pl.multiple_of(visit[step] * tile, tile)
        total = jnp.dot(
            matrix_ref[pl.ds(first_row, tile), :], x_ref[...], preferred_element_type=F32
        )
        if flags is not None:
            block = visit[step] * (tile // BLK)
            total = jnp.concatenate(
                [
                    total[i * BLK : (i + 1) * BLK] * shown[block + i].astype(F32)
                    for i in range(tile // BLK)
                ]
            )
        if addend is not None:
            total = total + addend_ref[...]
        for index, ref in enumerate(out_refs):

            @pl.when((step >= starts[index]) & (step < starts[index + 1]))
            def _():
                ref[...] = total.astype(ref.dtype)

    def out_map(first, last):
        return lambda i, *_: (jnp.clip(i - first, 0, last - first - 1), 0)

    in_specs = [pl.BlockSpec(memory_space=pltpu.VMEM)] * (count + 1)
    operands = list(vectors) + [matrix]
    if addend is not None:
        in_specs.append(pl.BlockSpec((tile, width), lambda i, *_: (i, 0)))
        operands.append(addend)
    return pl.pallas_call(
        body,
        grid_spec=pltpu.PrefetchScalarGridSpec(
            num_scalar_prefetch=3,
            grid=(steps,),
            in_specs=in_specs,
            out_specs=[
                pl.BlockSpec((tile, width), out_map(starts[i], starts[i + 1]))
                for i in range(len(outs))
            ],
            scratch_shapes=[pltpu.VMEM((inner, width), BF16)] if gathered else [],
        ),
        out_shape=[jax.ShapeDtypeStruct((r, width), t) for r, t in outs],
        compiler_params=pltpu.CompilerParams(vmem_limit_bytes=KERNEL_VMEM),
        cost_estimate=pl.CostEstimate(
            flops=2 * rows * inner * width,
            transcendentals=0,
            bytes_accessed=4 * (rows + inner) * width,
        ),
        name="multiply",
    )(in_blocks, order, jnp.zeros((1,), jnp.int32) if flags is None else flags, *operands)


def multiply_back(matrix, vectors, in_blocks, order, outs, flags=None, addend=None):
    inner, columns = matrix.shape
    width = vectors[0].shape[0]
    steps = order.shape[0]
    tile = columns // steps
    in_size = inner // in_blocks.shape[0]
    mask_size = min(BLK, in_size)
    starts = [0]
    for out_columns, _ in outs:
        starts.append(starts[-1] + out_columns // tile)
    count = len(vectors)

    def body(places, visit, shown, *refs):
        vector_refs = refs[:count]
        matrix_ref = refs[count]
        addend_ref = refs[count + 1] if addend is not None else None
        y_ref = refs[-1]
        out_refs = refs[count + 1 + (addend is not None) : -1]
        step = pl.program_id(0)

        @pl.when(step == 0)
        def _():
            at = 0
            for ref in vector_refs:
                for part in range(ref.shape[1] // in_size):
                    if flags is None:
                        place = pl.multiple_of(places[at] * in_size, in_size)
                        y_ref[:, pl.ds(place, in_size)] = ref[:, part * in_size : (part + 1) * in_size]
                    else:
                        for inside in range(in_size // mask_size):
                            block = places[at] * (in_size // mask_size) + inside
                            place = pl.multiple_of(block * mask_size, mask_size)
                            start = part * in_size + inside * mask_size
                            held = ref[:, start : start + mask_size]
                            y_ref[:, pl.ds(place, mask_size)] = jnp.where(
                                shown[block] != 0, held, jnp.zeros_like(held)
                            )
                    at += 1

        first_column = pl.multiple_of(visit[step] * tile, tile)
        total = jnp.dot(
            y_ref[...], matrix_ref[:, pl.ds(first_column, tile)], preferred_element_type=F32
        )
        if addend is not None:
            total = total + addend_ref[...]
        for index, ref in enumerate(out_refs):

            @pl.when((step >= starts[index]) & (step < starts[index + 1]))
            def _():
                ref[...] = total.astype(ref.dtype)

    def out_map(first, last):
        return lambda i, *_: (0, jnp.clip(i - first, 0, last - first - 1))

    in_specs = [pl.BlockSpec(memory_space=pltpu.VMEM)] * (count + 1)
    operands = list(vectors) + [matrix]
    if addend is not None:
        in_specs.append(pl.BlockSpec((width, tile), lambda i, *_: (0, i)))
        operands.append(addend)
    return pl.pallas_call(
        body,
        grid_spec=pltpu.PrefetchScalarGridSpec(
            num_scalar_prefetch=3,
            grid=(steps,),
            in_specs=in_specs,
            out_specs=[
                pl.BlockSpec((width, tile), out_map(starts[i], starts[i + 1]))
                for i in range(len(outs))
            ],
            scratch_shapes=[pltpu.VMEM((width, inner), BF16)],
        ),
        out_shape=[jax.ShapeDtypeStruct((width, c), t) for c, t in outs],
        compiler_params=pltpu.CompilerParams(vmem_limit_bytes=KERNEL_VMEM),
        cost_estimate=pl.CostEstimate(
            flops=2 * columns * inner * width,
            transcendentals=0,
            bytes_accessed=4 * (columns + inner) * width,
        ),
        name="multiply_back",
    )(in_blocks, order, jnp.zeros((1,), jnp.int32) if flags is None else flags, *operands)


def flip(*values):
    count = len(values)
    columns = values[0].shape[1]
    tile = min(columns, 256)

    def body(*refs):
        at = 0
        for ref in refs[:count]:
            refs[-1][:, at : at + ref.shape[0]] = ref[...].T
            at += ref.shape[0]

    rows = sum(v.shape[0] for v in values)
    return pl.pallas_call(
        body,
        grid=(columns // tile,),
        in_specs=[pl.BlockSpec((v.shape[0], tile), lambda i: (0, i)) for v in values],
        out_specs=pl.BlockSpec((tile, rows), lambda i: (i, 0)),
        out_shape=jax.ShapeDtypeStruct((columns, rows), values[0].dtype),
        compiler_params=pltpu.CompilerParams(vmem_limit_bytes=4 << 20),
        cost_estimate=pl.CostEstimate(
            flops=0, transcendentals=0, bytes_accessed=4 * rows * columns
        ),
        name="flip",
    )(*values)


def listed(*values):
    return jnp.stack([jnp.asarray(v, jnp.int32) for v in values])


def spread(blocks, size, tile):
    parts = size // tile
    return (blocks[:, None] * parts + jnp.arange(parts, dtype=jnp.int32)[None]).reshape(-1)


def add_all(own, *others):
    total = own
    for other in others:
        total = total + other.astype(F32)
    return total


def both_rows(values):
    return values.astype(F32) + swap_x(values).astype(F32)


def reduce_z(far_send, near_send, far_own, own):
    passed = add_all(far_own, swap_z(far_send, 1)).astype(BF16)
    return add_all(own, swap_z(near_send, 1), swap_z(passed, 3))


def gather_z(piece):
    across = swap_z(piece, 3)
    beside = swap_z(piece, 1)
    return [piece, beside, swap_z(across, 1), across]


def cut(values, count, axis):
    size = values.shape[axis] // count
    return [lax.slice_in_dim(values, i * size, (i + 1) * size, axis=axis) for i in range(count)]


def paired(parts, axis):
    return [jnp.concatenate(parts[:2], axis=axis), jnp.concatenate(parts[2:], axis=axis)]


def reduce_core_z(send, own, axis):
    total = add_all(own, swap_core(send))
    far_send, near_send, far_own, own = cut(total, 4, axis)
    return reduce_z(far_send.astype(BF16), near_send.astype(BF16), far_own, own)


def reduce_core_y_z(send, own, axis):
    kept, sent = cut(add_all(own, swap_core(send)), 2, axis)
    passed, final = [
        add_all(k, swap_y(s.astype(BF16))) for k, s in zip(cut(kept, 2, axis), cut(sent, 2, axis))
    ]
    far_send, near_send = cut(passed, 2, axis)
    far_own, own = cut(final, 2, axis)
    return reduce_z(far_send.astype(BF16), near_send.astype(BF16), far_own, own)


def gather_z_core(piece, axis):
    parts = paired(gather_z(piece), axis)
    return parts + [swap_core(p) for p in parts]


def gather_z_y_core(piece, axis):
    parts = paired(gather_z(piece), axis)
    parts = parts + [swap_y(p) for p in parts]
    return parts + [swap_core(p) for p in parts]


def solve(
    inverse_quarter,
    inverse_half,
    inverse_root,
    quarter_to_half,
    quarter_to_root,
    half_to_root,
    right_quarter,
    right_half,
    right_root,
    row_flags,
):
    sub_index = lax.axis_index("sub")
    column = lax.axis_index("col")
    low = sub_index % 2
    high = sub_index // 2
    zs = range(4)
    visit_z = (2, 1, 3, 0)
    mask_half, mask_root, mask_upper = row_flags[0], row_flags[1], row_flags[2]
    panel_rows, panel_columns = quarter_to_half.shape
    piece_rows = panel_rows // 2
    panel_tile = min(piece_rows, 512)

    col_blocks = listed(*[column ^ d for d in zs])
    col_visit = listed(*[column ^ d for d in visit_z])
    low_blocks = listed(low, low ^ 1)
    high_blocks = listed(high, high ^ 1)
    low_visit = spread(listed(low ^ 1, low), piece_rows, panel_tile)
    high_visit = spread(listed(high ^ 1, high), piece_rows, panel_tile)
    half_blocks = listed(*[(low ^ a) * 4 + (column ^ d) for a in (0, 1) for d in zs])
    half_visit = listed(*[(low ^ a) * 4 + (column ^ d) for a in (1, 0) for d in visit_z])
    root_place = lambda a, b, d: ((low ^ a) * 2 + (high ^ b)) * 4 + (column ^ d)
    root_visit = listed(*[root_place(a, b, d) for a in (1, 0) for b in (0, 1) for d in visit_z])
    root_blocks = listed(*[root_place(a, b, d) for a in (0, 1) for b in (0, 1) for d in zs])
    one = jnp.zeros((1,), jnp.int32)
    in_turn = lambda columns: jnp.arange(columns // min(columns, 512), dtype=jnp.int32)

    rows = inverse_quarter.shape[0]
    piece = rows // 4
    held = fetch(inverse_quarter, pieces=col_visit[:2], size=piece)
    pair = jnp.arange(4, dtype=jnp.int32)
    sends = [multiply(held, [x], one, pair, [(piece, BF16)] * 2) for x in right_quarter]
    held = fetch(inverse_quarter, sends[-1][0], pieces=col_visit[2:], size=piece)
    parts = [
        send + multiply(held, [x], one, pair, [(piece, F32)] * 2)
        for x, send in zip(right_quarter, sends)
    ]
    quarter_piece = [reduce_z(*p).astype(BF16) for p in parts]
    held = fetch(quarter_to_half, quarter_piece[0])
    quarter_parts = [gather_z(p) for p in quarter_piece]

    parts = [
        multiply(
            held, x, col_blocks, low_visit, [(piece_rows, BF16), (piece_rows, F32)], flags=mask_half
        )
        for x in quarter_parts
    ]
    held = fetch(inverse_half, parts[0][0])
    half_right = [
        (r.astype(F32) - both_rows(add_all(own, swap_core(send)).astype(BF16))).astype(BF16)
        for r, (send, own) in zip(right_half, parts)
    ]
    rows = inverse_half.shape[0]
    parts = [
        multiply(held, [x], one, half_visit, [(rows // 2, BF16), (rows // 2, F32)])
        for x in half_right
    ]
    held_root = fetch(quarter_to_root, parts[-1][0])
    root_part = [
        multiply(held_root, x, col_blocks, high_visit, [(panel_rows, F32)], flags=mask_root)[0]
        for x in quarter_parts
    ]
    half_piece = [reduce_core_z(send, own, 0).astype(BF16) for send, own in parts]
    held = fetch(half_to_root, half_piece[0], root_part[-1])
    half_parts = [gather_z_core(p, 0) for p in half_piece]

    parts = [
        multiply(
            held, x, half_blocks, high_visit, [(piece_rows, BF16), (piece_rows, F32)],
            flags=mask_upper, addend=early,
        )
        for x, early in zip(half_parts, root_part)
    ]
    held_root = fetch(inverse_root, parts[0][0])
    root_right = [
        (r.astype(F32) - both_rows(add_all(own, swap_y(send)).astype(BF16))).astype(BF16)
        for r, (send, own) in zip(right_root, parts)
    ]

    rows = inverse_root.shape[0]
    parts = [
        multiply(held_root, [x], one, root_visit, [(rows // 2, BF16), (rows // 2, F32)])
        for x in root_right
    ]

    root_piece = [flip(reduce_core_y_z(send, own, 0).astype(BF16)) for send, own in parts]
    held_root = fetch(inverse_root, root_piece[0])
    root_parts = [gather_z_y_core(p, 1) for p in root_piece]
    columns = inverse_root.shape[1]
    parts = [
        multiply_back(held_root, y, root_blocks, in_turn(columns), [(columns, BF16)])[0]
        for y in root_parts
    ]
    held = fetch(half_to_root, parts[0])
    root_solution = [both_rows(p).astype(BF16) for p in parts]
    root_pieces = [[p, swap_y(p)] for p in root_solution]

    parts = [
        multiply_back(
            held, y, high_blocks, half_visit,
            [(panel_columns // 2, BF16), (panel_columns // 2, F32)], flags=mask_upper,
        )
        for y in root_pieces
    ]
    held_root = fetch(quarter_to_root, parts[0][0])
    root_out, *flipped = lax.optimization_barrier(
        (flip(*root_solution), *[flip(p) for p in half_piece])
    )
    update = [
        (p.astype(F32) - reduce_core_z(send, own, 1)).astype(BF16)
        for p, (send, own) in zip(flipped, parts)
    ]
    update_parts = [gather_z_core(p, 1) for p in update]
    quarter_back = [
        multiply_back(held_root, y, high_blocks, col_visit, [(panel_columns, F32)], flags=mask_root)[0]
        for y in root_pieces
    ]

    columns = inverse_half.shape[1]
    held = fetch(inverse_half, quarter_back[0])
    parts = [
        multiply_back(held, y, half_blocks, in_turn(columns), [(columns, BF16)])[0]
        for y in update_parts
    ]
    held_root = fetch(quarter_to_half, parts[0])
    half_solution = [both_rows(p).astype(BF16) for p in parts]
    half_pieces = [[p, swap_core(p)] for p in half_solution]

    piece = panel_columns // 4
    parts = [
        multiply_back(
            held_root, y, low_blocks, col_visit, [(piece, BF16)] * 2 + [(piece, F32)] * 2,
            flags=mask_half, addend=early,
        )
        for y, early in zip(half_pieces, quarter_back)
    ]
    half_out, *flipped = lax.optimization_barrier(
        (flip(*half_solution), *[flip(q) for q in quarter_piece])
    )
    update = [
        (q.astype(F32) - reduce_z(*p)).astype(BF16) for q, p in zip(flipped, parts)
    ]
    held = fetch(inverse_quarter, update[0])
    columns = inverse_quarter.shape[1]
    quarter = [
        multiply_back(held, gather_z(y), col_blocks, in_turn(columns), [(columns, F32)])[0]
        for y in update
    ]
    return quarter, half_out, root_out


def pick(values, index):
    return lax.dynamic_index_in_dim(values, index, 0, keepdims=False)


def is_power_of_two(count):
    return count & (count - 1) == 0


def scatter_sum(partial, axis):
    count = lax.axis_size(axis)
    own = lax.axis_index(axis)
    pieces = partial.reshape(count, partial.shape[0] // count, partial.shape[1])
    total = pick(pieces, own)
    for distance in range(1, count):
        total = total + swap(pick(pieces, own ^ distance).astype(BF16), axis, distance).astype(F32)
    return total


def gather(piece, axis):
    count = lax.axis_size(axis)
    own = lax.axis_index(axis)
    whole = jnp.zeros((count,) + piece.shape, piece.dtype)
    whole = lax.dynamic_update_index_in_dim(whole, piece, own, 0)
    for distance in range(1, count):
        whole = lax.dynamic_update_index_in_dim(
            whole, swap(piece, axis, distance), own ^ distance, 0
        )
    return whole.reshape((count * piece.shape[0],) + piece.shape[1:])


def pair_scatter(halves, bit_value, axis, distance):
    own_piece = pick(halves, bit_value)
    other_piece = pick(halves, 1 - bit_value)
    return own_piece + swap(other_piece.astype(BF16), axis, distance).astype(F32)


def pair_gather(piece, bit_value, axis, distance):
    other = swap(piece, axis, distance)
    return jnp.where(bit_value == 0, jnp.stack([piece, other]), jnp.stack([other, piece]))


def sum_rows(values):
    if lax.axis_size("row") != 2:
        return lax.psum(values, "row")
    sent = values.astype(BF16)
    return sent.astype(F32) + swap(sent, "row", 1).astype(F32)


def project(matrix, vector):
    halves, height, inner = matrix.shape
    flat = jnp.dot(
        matrix.reshape(halves * height, inner), vector, preferred_element_type=F32
    )
    return flat.reshape(halves, height, vector.shape[1])


def transposed(matrix, vector):
    return lax.dot_general(
        matrix, vector, (((0,), (0,)), ((), ())), preferred_element_type=F32
    )


def project_back(matrix, pieces):
    return transposed(
        matrix.reshape(-1, matrix.shape[2]), pieces.reshape(-1, pieces.shape[2])
    )


def halve(values):
    return values.reshape(2, values.shape[0] // 2, values.shape[1])


def join(values):
    return values.reshape(-1, values.shape[2])


def final_sum(values):
    if lax.axis_size("row") != 2:
        return lax.psum_scatter(values, "row", scatter_dimension=1, tiled=True)
    own = lax.axis_index("row")
    width = values.shape[1] // 2
    mine = lax.dynamic_slice_in_dim(values, own * width, width, 1)
    sent = lax.dynamic_slice_in_dim(values, (1 - own) * width, width, 1)
    return mine + swap(sent.astype(BF16), "row", 1).astype(F32)


def solve_plain(
    inverse_quarter,
    inverse_half,
    inverse_root,
    quarter_to_half,
    quarter_to_root,
    half_to_root,
    right_quarter,
    right_half,
    right_root,
    masking,
):
    sub_index = lax.axis_index("sub")
    low_bit = sub_index % 2
    high_bit = sub_index // 2
    mask_half, mask_root, mask_upper = masking[0], masking[1], masking[2]

    quarter_partial = jnp.dot(inverse_quarter, right_quarter, preferred_element_type=F32)
    quarter_piece = scatter_sum(quarter_partial, "col").astype(BF16)
    solved_quarter = gather(quarter_piece, "col")

    half_part = project(quarter_to_half, solved_quarter) * mask_half
    half_terms = sum_rows(pair_scatter(half_part, low_bit, "sub", 1))
    half_right = (right_half.astype(F32) - half_terms).astype(BF16)
    root_part = project(quarter_to_root, solved_quarter) * mask_root

    half_partial = jnp.dot(inverse_half, half_right, preferred_element_type=F32)
    half_partial = pair_scatter(halve(half_partial), low_bit, "sub", 1)
    half_piece = scatter_sum(half_partial, "col").astype(BF16)
    solved_half = join(pair_gather(gather(half_piece, "col"), low_bit, "sub", 1))

    upper_part = project(half_to_root, solved_half) * mask_upper
    root_terms = sum_rows(pair_scatter(upper_part + root_part, high_bit, "sub", 2))
    root_right = (right_root.astype(F32) - root_terms).astype(BF16)

    root_partial = jnp.dot(inverse_root, root_right, preferred_element_type=F32)
    root_partial = pair_scatter(halve(root_partial), low_bit, "sub", 1)
    root_partial = pair_scatter(halve(root_partial), high_bit, "sub", 2)
    root_piece = scatter_sum(root_partial, "col").astype(BF16)
    solved_root = join(pair_gather(gather(root_piece, "col"), high_bit, "sub", 2))
    solved_root = join(pair_gather(solved_root, low_bit, "sub", 1))

    root_solution = sum_rows(transposed(inverse_root, solved_root)).astype(BF16)
    root_pieces = pair_gather(root_solution, high_bit, "sub", 2)

    upper_back = project_back(half_to_root, root_pieces * mask_upper.astype(BF16))
    upper_back = pair_scatter(halve(upper_back), low_bit, "sub", 1)
    upper_total = scatter_sum(upper_back, "col")
    half_update_piece = (half_piece.astype(F32) - upper_total).astype(BF16)
    half_update = join(pair_gather(gather(half_update_piece, "col"), low_bit, "sub", 1))
    quarter_back = project_back(quarter_to_root, root_pieces * mask_root.astype(BF16))

    half_solution = sum_rows(transposed(inverse_half, half_update)).astype(BF16)
    half_pieces = pair_gather(half_solution, low_bit, "sub", 1)

    quarter_back = quarter_back + project_back(
        quarter_to_half, half_pieces * mask_half.astype(BF16)
    )
    quarter_total = scatter_sum(quarter_back, "col")
    quarter_update_piece = (quarter_piece.astype(F32) - quarter_total).astype(BF16)
    quarter_update = gather(quarter_update_piece, "col")
    return transposed(inverse_quarter, quarter_update), half_solution, root_solution


def per_device(
    inverse_quarter,
    inverse_half,
    inverse_root,
    quarter_to_half,
    quarter_to_root,
    half_to_root,
    right_quarter,
    right_half,
    right_root,
    row_blocks,
):
    sub_index = lax.axis_index("sub")
    column_index = lax.axis_index("col")
    block_count = quarter_to_half.shape[2] // BLK
    row_flags = lax.dynamic_slice(
        row_blocks,
        (jnp.int32(0), sub_index, jnp.int32(0), column_index * block_count),
        (3, 1, 2, block_count),
    )[:, 0]
    smallest = min(inverse_quarter.shape[1] // 4, inverse_half.shape[1] // 8, inverse_root.shape[0] // 16)
    if (lax.axis_size("row"), lax.axis_size("col")) != (2, 4) or smallest % 128:
        quarter, half, root = solve_plain(
            inverse_quarter[0],
            inverse_half[0],
            inverse_root,
            quarter_to_half[0],
            quarter_to_root[0],
            half_to_root[0],
            right_quarter[0],
            right_half[0],
            right_root,
            jnp.repeat(row_flags, BLK, axis=2).astype(F32)[:, :, :, None],
        )
        return (final_sum(quarter)[None], half[None], root)
    panels = [p[0].reshape(-1, p.shape[3]) for p in (quarter_to_half, quarter_to_root, half_to_root)]
    quarter, half, root = solve(
        inverse_quarter[0],
        inverse_half[0],
        inverse_root,
        *panels,
        jnp.split(right_quarter[0], STREAMS, axis=1),
        jnp.split(right_half[0], STREAMS, axis=1),
        jnp.split(right_root, STREAMS, axis=1),
        row_flags.reshape(3, -1),
    )
    low_side, high_side = jnp.split(quarter[0], 2) if STREAMS == 1 else quarter
    first = lax.axis_index("row") == 0
    own = jnp.where(first, low_side, high_side)
    send = jnp.where(first, high_side, low_side).astype(BF16)
    quarter = (own + swap_x(send).astype(F32)).T
    return (quarter[None], half[None], root)


def solution(mesh):
    placed = (
        P("sub", "row", "col"),
        P("sub", "row", "col"),
        P("row", ("sub", "col")),
        P("sub", None, "col", "row"),
        P("sub", None, "col", "row"),
        P("sub", None, "col", "row"),
        P("sub", "col", None),
        P("sub", "col", None),
        P(("sub", "col"), None),
        P(),
    )
    return jax.shard_map(
        per_device,
        mesh=mesh,
        in_specs=placed,
        out_specs=(P("sub", "col", "row"), P("sub", "col", None), P(("sub", "col"), None)),
        check_vma=False,
    )
```
